32 devices in a mesh: heads: 2 (over y), seq: 16 (over z, x, core).
Axes of the slice: x: 2, y: 2, z: 4, core: 2. Of those that a mesh axis runs over, the one named last changes fastest.
Arguments:
- signal: bfloat16 [2048, 1280], P('seq', 'heads'), may hold values from -6 to 6
- b_in: bfloat16 [2048, 128], P('seq'), may hold values from -1.75 to 1.75
- c_in: bfloat16 [2048, 128], P('seq'), may hold values from -1.75 to 1.75
- step: float32 [20, 2048], P('heads', 'seq'), may hold values from 0.008 to 0.03
- decay_log: float32 [20, 2048], P('heads', 'seq'), may hold values from -2.3 to 0
- level_weight: float32 [8, 20, 2048], P(None, 'heads', 'seq'), may hold values from 0.02 to 4
- skip: float32 [20], P('heads'), may hold values from 0.5 to 1.5
- grad_out: bfloat16 [2048, 1280], P('seq', 'heads'), may hold values from -6 to 6
- state_cotangent: float32 [20, 128, 64], P('heads'), may hold values from -12 to 12
Outputs:
- output: bfloat16 [2048, 1280], P('seq', 'heads')
- dx: bfloat16 [2048, 1280], P('seq', 'heads')
- db: bfloat16 [2048, 128], P('seq')
- dc: bfloat16 [2048, 128], P('seq')
The draws below stay inside these ranges and needn't reach their ends.
All inputs are finite; a program needn't handle non-finite values.
Results may differ from the reference program's by a relative error of at most 0.001.
Values may be sent and summed in bfloat16 or wider, within the bound.
A program may use at most 64 MiB of HBM per device.

```python
import math
import jax
import jax.numpy as jnp
from jax import lax

P_SIZE = 64
N = 128
HEADS = 20
TOK_DEV = 128
TOKENS = 2048
LEVELS = 8
N_SEQ = 16


def draw_decay_log(key, part):
    key_slow, key_fast, key_selector, key_rough, key_where, key_size = jax.random.split(key, 6)
    share = 0.5
    slow = jax.random.uniform(key_slow, (HEADS,)) < share
    fast_rate = jnp.exp(jax.random.uniform(key_fast, (HEADS,), jnp.float32, jnp.log(1.0 / 50.0), jnp.log(1.0 / 30.0)))
    slow_rate = jax.random.uniform(key_selector, (HEADS,), jnp.float32, 0.2, 0.6) / TOKENS
    decay_speed = jnp.where(slow, slow_rate, fast_rate)
    coarse_level = jax.random.uniform(key_rough, (HEADS, TOKENS), jnp.float32, 0.5, 1.5)
    spots = jax.random.randint(key_where, (HEADS, 3), 0, TOKENS)
    shard_lengths = jax.random.uniform(key_size, (HEADS, 3), jnp.float32, 0.22, 0.69)
    positions = jnp.arange(TOKENS, dtype=jnp.int32)
    match_flags = (positions[None, None, :] == spots[:, :, None]).astype(jnp.float32)
    spike_amplitude = jnp.sum(match_flags * shard_lengths[:, :, None], axis=1)
    return (-(decay_speed[:, None] * coarse_level) - spike_amplitude).astype(jnp.float32)


def draw_level_weight(key, part):
    base = jax.random.uniform(key, (LEVELS, HEADS, TOKENS), jnp.float32, 0.5, 2.0)
    depth = jnp.arange(LEVELS, dtype=jnp.float32)[:, None, None]
    return (base * jnp.exp(-0.5 * jnp.log(2.0) * depth)).astype(jnp.float32)


def block_scale(rng, extent, cuts, least, high):
    level, own = 1.0, jax.random.fold_in(rng, 6)
    for position, blocks in cuts:
        heights = jnp.exp(jax.random.uniform(jax.random.fold_in(own, position), (blocks,), jnp.float32, least / len(cuts), high / len(cuts)))
        level = level * jnp.repeat(heights, extent[position] // blocks).reshape([-1 if axis == position else 1 for axis in range(len(extent))])
    return level


def normal_values(stream_key, dims, spread, limit, pieces=(), held_as=jnp.bfloat16):
    loudness = block_scale(stream_key, dims, pieces, -0.22, 0.18) if pieces else 1.0
    drawn = jax.random.normal(stream_key, dims, jnp.float32) * spread * loudness
    return jnp.minimum(jnp.maximum(drawn, -limit), limit).astype(held_as)


def setup_inputs(seed: int = 0) -> dict:
    splits = jax.random.split(jax.random.key(seed), 10)
    signal = normal_values(splits[0], (TOKENS, HEADS * P_SIZE), 1.0, 6.0, ((0, 16), (1, 2)))
    b_in = normal_values(splits[1], (TOKENS, N), 0.3, 1.75, ((0, 16),))
    c_in = normal_values(splits[2], (TOKENS, N), 0.3, 1.75, ((0, 16),))
    step = jnp.clip(jnp.exp(math.log(0.03) - 1.3217558 * jax.random.uniform(splits[3], (HEADS, TOKENS), jnp.float32) ** block_scale(splits[3], (HEADS, TOKENS), ((0, 2), (1, 16)), -0.2, 0.2)), 0.008, 0.03)
    decay_log = draw_decay_log(jax.random.fold_in(splits[9], 71), 0)
    level_weight = draw_level_weight(jax.random.fold_in(splits[9], 71), 0)
    skip = jnp.clip(0.5 + 1.0 * jax.random.uniform(splits[6], (HEADS,), jnp.float32) ** block_scale(splits[6], (HEADS,), ((0, 2),), -0.2, 0.2), 0.5, 1.5)
    grad_out = normal_values(splits[7], (TOKENS, HEADS * P_SIZE), 1.0, 6.0, ((0, 16), (1, 2)))
    state_cotangent = normal_values(splits[8], (HEADS, N, P_SIZE), 2.0, 12.0, ((0, 2),), jnp.float32)
    return {"signal": signal, "b_in": b_in, "c_in": c_in, "step": step, "decay_log": decay_log, "level_weight": level_weight, "skip": skip, "grad_out": grad_out, "state_cotangent": state_cotangent}


HIGH = lax.Precision.HIGHEST


def forward_one(args):
    xd, bd, cd, sd, cum_d = args
    tokens = xd.shape[0]
    rows = lax.broadcasted_iota(jnp.int32, (tokens, tokens), 0)
    cols = lax.broadcasted_iota(jnp.int32, (tokens, tokens), 1)
    lower = (rows >= cols)[None]
    diff = cum_d[:, :, None] - cum_d[:, None, :]
    weight = jnp.where(lower, jnp.exp(jnp.where(lower, diff, 0.0)), 0.0)
    scores = jnp.dot(cd, bd.T, precision=HIGH)
    mixing = scores[None] * weight
    inputs = sd.T[:, :, None] * xd
    y_local = jnp.einsum("hts,shp->thp", mixing, inputs, precision=HIGH)
    tail = jnp.exp(cum_d[:, -1:] - cum_d)
    state = jnp.einsum("hs,sn,shp->hnp", tail, bd, inputs, precision=HIGH)
    return y_local, state


def level_one(args):
    coef_d, cd, dyd, level_d = args
    y_add = jnp.einsum("ht,tn,hnp->thp", coef_d, cd, level_d, precision=HIGH)
    dc_add = jnp.einsum("ht,thp,hnp->tn", coef_d, dyd, level_d, precision=HIGH)
    return y_add, dc_add


def grad_one(args):
    coef_d, cd, dyd = args
    return jnp.einsum("ht,tn,thp->hnp", coef_d, cd, dyd, precision=HIGH)


def backward_one(args):
    xd, bd, cd, sd, cum_d, dyd, state_grad, skip_all = args
    tokens = xd.shape[0]
    rows = lax.broadcasted_iota(jnp.int32, (tokens, tokens), 0)
    cols = lax.broadcasted_iota(jnp.int32, (tokens, tokens), 1)
    lower = (rows >= cols)[None]
    diff = cum_d[:, :, None] - cum_d[:, None, :]
    weight = jnp.where(lower, jnp.exp(jnp.where(lower, diff, 0.0)), 0.0)
    scores = jnp.dot(cd, bd.T, precision=HIGH)
    mixing = scores[None] * weight
    inputs = sd.T[:, :, None] * xd
    tail = jnp.exp(cum_d[:, -1:] - cum_d)
    mix_grad = jnp.einsum("thp,shp->hts", dyd, inputs, precision=HIGH)
    score_grad = jnp.sum(mix_grad * weight, axis=0)
    in_grad = jnp.einsum("hts,thp->shp", mixing, dyd, precision=HIGH)
    in_grad = in_grad + jnp.einsum("hs,sn,hnp->shp", tail, bd, state_grad, precision=HIGH)
    dc_part = jnp.dot(score_grad, bd, precision=HIGH)
    db_part = jnp.dot(score_grad.T, cd, precision=HIGH)
    db_part = db_part + jnp.einsum("hs,shp,hnp->sn", tail, inputs, state_grad, precision=HIGH)
    dx_part = skip_all[None, :, None] * dyd + sd.T[:, :, None] * in_grad
    return dx_part, db_part, dc_part


def reference(signal, b_in, c_in, step, decay_log, level_weight, skip, grad_out, state_cotangent):
    count = N_SEQ
    tok = TOK_DEV
    xs = signal.astype(jnp.float32).reshape(count, tok, HEADS, P_SIZE)
    dys = grad_out.astype(jnp.float32).reshape(count, tok, HEADS, P_SIZE)
    bs = b_in.astype(jnp.float32).reshape(count, tok, N)
    cs = c_in.astype(jnp.float32).reshape(count, tok, N)
    steps = step.reshape(HEADS, count, tok).transpose(1, 0, 2)
    cums = jnp.cumsum(decay_log.reshape(HEADS, count, tok), axis=2).transpose(1, 0, 2)
    lams = level_weight.reshape(LEVELS, HEADS, count, tok).transpose(2, 0, 1, 3)
    depth = N_SEQ.bit_length() - 1
    y_local, states = lax.map(forward_one, (xs, bs, cs, steps, cums))
    windows = jnp.arange(count, dtype=jnp.int32)
    totals = states
    decay_sum = cums[:, :, -1]
    offset = jnp.zeros((count, HEADS), jnp.float32)
    y_levels = jnp.zeros((count, tok, HEADS, P_SIZE), jnp.float32)
    dc_levels = jnp.zeros((count, tok, N), jnp.float32)
    records = []
    for bit in range(depth):
        partner = jnp.bitwise_xor(windows, jnp.int32(1 << bit))
        upper = (jnp.bitwise_and(jnp.right_shift(windows, bit), 1) == 1)[:, None]
        far_total = totals[partner]
        far_decay = decay_sum[partner]
        level = jnp.where(upper[:, :, None, None], jnp.exp(offset)[:, :, None, None] * far_total, 0.0)
        coef = lams[:, bit] * jnp.exp(cums)
        y_add, dc_add = lax.map(level_one, (coef, cs, dys, level))
        y_levels = y_levels + y_add
        dc_levels = dc_levels + dc_add
        records.append((upper, decay_sum, far_decay, offset, coef, partner))
        totals = jnp.where(upper[:, :, None, None], totals + jnp.exp(decay_sum)[:, :, None, None] * far_total,
                           far_total + jnp.exp(far_decay)[:, :, None, None] * totals)
        offset = jnp.where(upper, offset + far_decay, offset)
        decay_sum = decay_sum + far_decay
    first = (windows == 0)[:, None, None, None]
    carry = jnp.where(first, state_cotangent[None].astype(jnp.float32), jnp.float32(0.0)) * jnp.ones_like(states)
    for bit in reversed(range(depth)):
        upper, own_decay, far_decay, offset_k, coef, partner = records[bit]
        grad_level = lax.map(grad_one, (coef, cs, dys))
        send = jnp.where(upper[:, :, None, None],
                         jnp.exp(own_decay)[:, :, None, None] * carry + jnp.exp(offset_k)[:, :, None, None] * grad_level,
                         carry)
        keep = jnp.where(upper[:, :, None, None], carry, jnp.exp(far_decay)[:, :, None, None] * carry)
        carry = keep + send[partner]
    skips = jnp.broadcast_to(skip[None], (count, HEADS))
    dx_all, db_all, dc_all = lax.map(backward_one, (xs, bs, cs, steps, cums, dys, carry, skips))
    output = (y_local + y_levels + skip[None, None, :, None] * xs).astype(jnp.bfloat16)
    output = output.reshape(count * tok, HEADS * P_SIZE)
    dx = dx_all.astype(jnp.bfloat16).reshape(count * tok, HEADS * P_SIZE)
    db = db_all.astype(jnp.bfloat16).reshape(count * tok, N)
    dc = (dc_all + dc_levels).astype(jnp.bfloat16).reshape(count * tok, N)
    return output, dx, db, dc
```

```python
import functools

import jax
import jax.numpy as jnp
from jax import lax
from jax.experimental import pallas as pl
from jax.experimental.pallas import tpu as pltpu
from jax.sharding import PartitionSpec as P

MESH = pl.DeviceIdType.MESH
HIGH = lax.Precision.HIGHEST
F32 = jnp.float32
BF16 = jnp.bfloat16


def split(v):
    hi = v.astype(BF16)
    return hi, (v - hi.astype(F32)).astype(BF16)


def dot(a, b, ca, cb):
    return lax.dot_general(a, b, (((ca,), (cb,)), ((), ())), preferred_element_type=F32)


def kernel(
    n, depth, nh, heads, width, has_rest,
    x_ref, b_ref, c_ref, step_ref, decay_ref, lw_ref, skip_ref, dy_ref, cot_ref,
    y_out, dx_out, db_out, dc_out,
    gall, s_buf, t1, f, tq, g, rc, gh, rx, g1, r0, cs, cr, dt,
    v_hi, v_lo, coefx, u_hi, u_lo, tsx, y_acc, dx_acc, sg, dcl, hx,
    ssem, rsem, gs_sem, gr_sem, hs_sem, hr_sem,
):
    me = lax.axis_index("seq")
    mh = lax.axis_index("heads")
    tokens = x_ref.shape[0]
    rows = b_ref.shape[1]
    half, quarter = rows // 2, rows // 4
    psize = width // heads
    core = me % 2
    xbit = (me // 2) % 2
    half_own = pl.multiple_of(core * half, half)
    half_other = pl.multiple_of((1 - core) * half, half)
    q_own = pl.multiple_of(core * half + xbit * quarter, quarter)

    def bit(k):
        return (me // (1 << k)) % 2

    def partner(k):
        return me + (1 << k) * (1 - 2 * bit(k))

    barrier = pltpu.get_barrier_semaphore()

    def greet(j, carry):
        pl.semaphore_signal(barrier, inc=1, device_id={"seq": (me + j) % n}, device_id_type=MESH)
        return carry

    lax.fori_loop(1, n, greet, 0)
    for j in range(1, nh):
        pl.semaphore_signal(barrier, inc=1, device_id={"heads": (mh + j) % nh}, device_id_type=MESH)

    pending = []

    def copy(idx, src, dst, k):
        return pltpu.make_async_remote_copy(
            src_ref=src, dst_ref=dst, send_sem=ssem.at[idx], recv_sem=rsem.at[idx],
            device_id={"seq": partner(k)}, device_id_type=MESH,
        )

    names = {}

    def send(name, src, dst, k, when=None):
        idx = names.setdefault(name, len(names))
        cp = copy(idx, src, dst, k)
        pending.append((cp, when))
        if when is None:
            cp.start()
        else:
            pl.when(when)(cp.start)

    def recv(name, dst, k, when=None):
        idx = names[name]
        cp = copy(idx, dst, dst, k)
        if when is None:
            cp.wait_recv()
        else:
            pl.when(when)(cp.wait_recv)

    hpad = -(-heads // 16) * 16
    hrow = lax.broadcasted_iota(jnp.int32, (hpad, width), 0)
    hcol = lax.broadcasted_iota(jnp.int32, (hpad, width), 1)
    e1 = jnp.where((hcol >= hrow * psize) & (hcol < (hrow + 1) * psize), 1.0, 0.0).astype(BF16)
    e3 = jnp.concatenate([e1, e1, e1], axis=0)

    def pad(v):
        return jnp.concatenate([v, jnp.zeros((hpad - heads, v.shape[1]), F32)], axis=0)

    def expand(v):
        p0 = v.astype(BF16)
        rest = v - p0.astype(F32)
        p1 = rest.astype(BF16)
        p2 = (rest - p1.astype(F32)).astype(BF16)
        return dot(jnp.concatenate([p0, p1, p2], axis=0), e3, 0, 0)

    ti = lax.broadcasted_iota(jnp.int32, (tokens, tokens), 0)
    tj = lax.broadcasted_iota(jnp.int32, (tokens, tokens), 1)
    lower = ti >= tj
    step = pad(step_ref[...])
    cum = jnp.dot(pad(decay_ref[...]), jnp.where(ti <= tj, 1.0, 0.0), precision=HIGH,
                  preferred_element_type=F32)
    gall[me] = expand(cum)[tokens - 1:tokens, :]

    x = x_ref[...]
    dy = dy_ref[...]
    b = b_ref[...]
    c = c_ref[...]

    pl.semaphore_wait(barrier, n - 1 + nh - 1)

    def share(j, carry):
        pltpu.make_async_remote_copy(
            src_ref=gall.at[me], dst_ref=gall.at[me], send_sem=gs_sem, recv_sem=gr_sem,
            device_id={"seq": (me + j) % n}, device_id_type=MESH,
        ).start()
        return carry

    lax.fori_loop(1, n, share, 0)

    tail = jnp.exp(cum[:, tokens - 1:tokens] - cum)
    ts = expand(tail * step)
    tsx[...] = ts
    uh, ul = split(ts * x.astype(F32))
    u_hi[...] = uh
    u_lo[...] = ul
    s_buf[...] = dot(b, uh, 0, 0) + dot(b, ul, 0, 0)
    send("F0", s_buf, f.at[0], 0)

    ecum = jnp.exp(cum)
    for k in range(depth):
        @pl.when(bit(k) == 1)
        def _():
            coef = expand(pad(lw_ref[k]) * ecum)
            coefx[k] = coef
            vh, vl = split(coef * dy.astype(F32))
            v_hi[k] = vh
            v_lo[k] = vl
            g[k] = dot(c, vh, 0, 0) + dot(c, vl, 0, 0)
        if k == 0:
            send("R0", g.at[0], r0, 0, bit(0) == 1)

    everything = pltpu.make_async_copy(gall.at[pl.ds(0, n - 1)], gall.at[pl.ds(0, n - 1)], gr_sem)
    everything.wait()
    windows = lax.broadcasted_iota(jnp.int32, (n, 1, width), 0)
    gv = gall[...]

    def retention(mask):
        return jnp.exp(jnp.sum(jnp.where(mask, gv, 0.0), axis=0))

    up = [retention((windows >> k) == ((me >> k) | 1)) for k in range(depth)]
    off = [None] + [retention(((windows >> k) == (me >> k)) & (windows < me)) for k in range(1, depth)]
    after = retention(windows > me)

    order = [1] + list(range(depth - 1, 1, -1))
    for k in order:
        @pl.when(bit(k) == 1)
        def _():
            g[k] = g[k] * off[k]
        send(("RC", k), g.at[k, pl.ds(half_other, half)], rc.at[k], 0, bit(k) == 1)

    def merge(k, own, far):
        is_up = bit(k) == 1
        return jnp.where(is_up, own + up[k] * far, far + up[k] * own)

    recv("F0", f.at[0], 0)
    own_rows = pl.ds(half_own, half)
    t1[...] = merge(0, s_buf[own_rows], f[0, own_rows])
    send("F1", t1, f.at[1, own_rows], 1)

    scores = dot(c, b, 1, 1)
    cum_t = cum.T
    left = lax.broadcasted_iota(jnp.int32, (tokens, 2 * psize), 1) < psize
    zero = jnp.zeros((tokens, 2 * psize), BF16)
    sg[...] = jnp.zeros_like(sg)

    def pair(p):
        lanes = slice(p * 2 * psize, (p + 1) * 2 * psize)
        xp, dyp = x[:, lanes], dy[:, lanes]
        xs = [jnp.where(left, xp, zero), jnp.where(left, zero, xp)]
        dys = [jnp.where(left, dyp, zero), jnp.where(left, zero, dyp)]
        his, los = [], []
        total = None
        for a in range(2):
            h = 2 * p + a
            diff = cum_t[:, h:h + 1] - cum[h:h + 1, :]
            w = jnp.where(lower, jnp.exp(jnp.where(lower, diff, 0.0)), 0.0) * step[h:h + 1, :]
            part = dot(dys[a], xs[a], 1, 1) * w
            total = part if total is None else total + part
            hi, lo = split(scores * w)
            his.append(hi)
            los.append(lo)
        sg[...] += total
        xcat = jnp.concatenate(xs, axis=0)
        dycat = jnp.concatenate(dys, axis=0)
        gain = jnp.where(left[:1], skip_ref[2 * p], skip_ref[2 * p + 1])
        y_acc[:, lanes] = (
            dot(jnp.concatenate(his, axis=1), xcat, 1, 0) + dot(jnp.concatenate(los, axis=1), xcat, 1, 0)
            + gain * xp.astype(F32))
        dx_acc[:, lanes] = (
            dot(jnp.concatenate(his, axis=0), dycat, 0, 0) + dot(jnp.concatenate(los, axis=0), dycat, 0, 0)
            + gain * dyp.astype(F32))

    pairs = list(range(heads // 2))

    def some(count):
        for _ in range(count):
            if pairs:
                pair(pairs.pop(0))

    some(1)
    for k in order:
        recv(("RC", k), rc.at[k], 0, bit(k) == 1)

        @pl.when(bit(k) == 1)
        def _():
            gh[k] = g[k, own_rows] + rc[k]
        if k >= 2:
            send(("RX", k), gh.at[k, pl.ds(pl.multiple_of((1 - xbit) * quarter, quarter), quarter)],
                 rx.at[k], 1, bit(k) == 1)
        else:
            send("R1X", gh.at[1], g1.at[own_rows], 1, bit(1) == 1)

    own_q = pl.ds(q_own, quarter)
    q_in_half = pl.ds(pl.multiple_of(xbit * quarter, quarter), quarter)
    recv("F1", f.at[1, own_rows], 1)
    tq[2] = merge(1, t1[q_in_half], f[1, own_q])
    top = depth - 1
    send(("F", 2), tq.at[2], f.at[2, own_q], 2, bit(2) == 0 if top == 2 else None)
    send("F1C", f.at[1, own_rows], f.at[1, own_rows], 0, bit(1) == 1)
    some(1)

    recv("R1X", g1.at[own_rows], 1, bit(1) == 0)
    send("R1A", g1.at[own_rows], g1.at[own_rows], 0, bit(1) == 0)
    cs[0] = jnp.zeros((quarter, width), F32)
    carry_slot = cs.at[0]

    def slab_grad(k):
        recv(("RX", k), rx.at[k], 1, bit(k) == 1)

    def level_full(k):
        recv(("FX", k), f.at[k, pl.ds(pl.multiple_of(core * half + (1 - xbit) * quarter, quarter), quarter)], 1,
             bit(k) == 1)
        send(("FC", k), f.at[k, own_rows], f.at[k, own_rows], 0, bit(k) == 1)

    carry = None
    for r in range(2, depth):
        kb = top - (r - 2)
        slab_grad(kb)
        is_up = bit(kb) == 1
        grad = jnp.where(is_up, gh[kb, q_in_half] + rx[kb], 0.0)
        if carry is None:
            cs[kb] = grad
            send(("C", kb), cs.at[kb], cr.at[kb], kb, is_up)
        else:
            cs[kb] = jnp.where(is_up, up[kb] * carry + grad, carry)
            send(("C", kb), cs.at[kb], cr.at[kb], kb)
        some(1)
        recv(("F", r), f.at[r, own_q], r, bit(r) == 1 if r == top else None)
        if r < top:
            tq[r + 1] = merge(r, tq[r], f[r, own_q])
            send(("F", r + 1), tq.at[r + 1], f.at[r + 1, own_q], r + 1, bit(r + 1) == 0 if r + 1 == top else None)
        send(("FX", r), f.at[r, own_q], f.at[r, own_q], 1, bit(r) == 1)
        if r > 2:
            level_full(r - 1)
        recv(("C", kb), cr.at[kb], kb, bit(kb) == 0 if kb == top else None)
        if carry is None:
            carry = jnp.where(is_up, 0.0, cr[kb])
        else:
            carry = jnp.where(is_up, carry, up[kb] * carry) + cr[kb]
    dt[own_q] = carry
    send("CX", dt.at[own_q], dt.at[own_q], 1)
    some(len(pairs))
    dcl[...] = dot(split(sg[...])[0], b, 1, 0) + dot(split(sg[...])[1], b, 1, 0)

    def use_level(k):
        @pl.when(bit(k) == 1)
        def _():
            level = f[k] if k == 0 else f[k] * off[k]
            lh, ll = split(level)
            y_acc[...] += coefx[k] * (dot(c, lh, 1, 0) + dot(c, ll, 1, 0))
            vh, vl = v_hi[k], v_lo[k]
            dcl[...] += dot(vh, lh, 1, 1) + dot(vh, ll, 1, 1) + dot(vl, lh, 1, 1)

    use_level(0)
    level_full(top)
    recv("F1C", f.at[1, pl.ds(half_other, half)], 0, bit(1) == 1)
    use_level(1)
    recv("CX", dt.at[pl.ds(pl.multiple_of(core * half + (1 - xbit) * quarter, quarter), quarter)], 1)
    send("CC", dt.at[own_rows], dt.at[own_rows], 0)
    for k in range(2, depth):
        recv(("FC", k), f.at[k, pl.ds(half_other, half)], 0, bit(k) == 1)
        use_level(k)
    y_out[...] = y_acc[...].astype(BF16)

    recv("R1A", g1.at[pl.ds(half_other, half)], 0, bit(1) == 0)
    recv("R0", r0, 0, bit(0) == 0)
    recv("CC", dt.at[pl.ds(half_other, half)], 0)
    cot = jnp.concatenate(
        [jnp.concatenate([cot_ref[2 * p], cot_ref[2 * p + 1]], axis=1) for p in range(heads // 2)], axis=1)
    ds_ = dt[...]
    ds_ = jnp.where(bit(1) == 1, ds_, up[1] * ds_ + g1[...])
    ds_ = jnp.where(bit(0) == 1, ds_, up[0] * ds_ + r0[...])
    ds_ = ds_ + after * cot
    dh, dl = split(ds_)
    uh, ul = u_hi[...], u_lo[...]
    sh, sl = split(sg[...])
    hx[mh, 0] = dcl[...]
    hx[mh, 1] = (dot(sh, c, 0, 0) + dot(sl, c, 0, 0)
                 + dot(uh, dh, 1, 1) + dot(uh, dl, 1, 1) + dot(ul, dh, 1, 1))

    def head_copy(j, slot):
        return pltpu.make_async_remote_copy(
            src_ref=hx.at[slot], dst_ref=hx.at[slot], send_sem=hs_sem.at[j], recv_sem=hr_sem.at[j],
            device_id={"heads": (mh + j) % nh}, device_id_type=MESH,
        )

    for j in range(1, nh):
        head_copy(j, mh).start()
    dx_out[...] = (dx_acc[...] + tsx[...] * (dot(b, dh, 1, 0) + dot(b, dl, 1, 0))).astype(BF16)
    for j in range(1, nh):
        head_copy(j, mh).wait_recv()
    dc, db = hx[0, 0], hx[0, 1]
    for v in range(1, nh):
        dc = dc + hx[v, 0]
        db = db + hx[v, 1]
    dc_out[...] = dc.astype(BF16)
    db_out[...] = db.astype(BF16)
    for j in range(1, nh):
        head_copy(j, mh).wait_send()
    for cp, when in pending:
        if when is None:
            cp.wait_send()
        else:
            pl.when(when)(cp.wait_send)
    pltpu.make_async_copy(gall.at[pl.ds(0, n - 1)], gall.at[pl.ds(0, n - 1)], gs_sem).wait()


def solution(mesh):
    n, nh = mesh.shape["seq"], mesh.shape["heads"]
    depth = n.bit_length() - 1

    def on_device(signal, b_in, c_in, step, decay_log, level_weight, skip, grad_out, state_cotangent):
        tokens, width = signal.shape
        heads = step.shape[0]
        rows = b_in.shape[1]
        half, quarter = rows // 2, rows // 4
        vm = lambda shape, dtype=F32: pltpu.VMEM(shape, dtype)
        count = 16 + 8 * depth
        spec = pl.BlockSpec(memory_space=pltpu.VMEM)
        return pl.pallas_call(
            functools.partial(kernel, n, depth, nh, heads, width, None),
            name="loglinear",
            out_shape=(
                jax.ShapeDtypeStruct((tokens, width), BF16),
                jax.ShapeDtypeStruct((tokens, width), BF16),
                jax.ShapeDtypeStruct((tokens, rows), BF16),
                jax.ShapeDtypeStruct((tokens, rows), BF16),
            ),
            in_specs=[spec] * 6 + [pl.BlockSpec(memory_space=pltpu.SMEM)] + [spec] * 2,
            out_specs=(spec,) * 4,
            scratch_shapes=[
                vm((n, 1, width)),
                vm((rows, width)),
                vm((half, width)),
                vm((depth, rows, width)),
                vm((depth, quarter, width)),
                vm((depth, rows, width)),
                vm((depth, half, width)),
                vm((depth, half, width)),
                vm((depth, quarter, width)),
                vm((rows, width)),
                vm((rows, width)),
                vm((depth, quarter, width)),
                vm((depth, quarter, width)),
                vm((rows, width)),
                vm((depth, tokens, width), BF16),
                vm((depth, tokens, width), BF16),
                vm((depth, tokens, width)),
                vm((tokens, width), BF16),
                vm((tokens, width), BF16),
                vm((tokens, width)),
                vm((tokens, width)),
                vm((tokens, width)),
                vm((tokens, tokens)),
                vm((tokens, rows)),
                vm((nh, 2, tokens, rows)),
                pltpu.SemaphoreType.DMA((count,)),
                pltpu.SemaphoreType.DMA((count,)),
                pltpu.SemaphoreType.DMA,
                pltpu.SemaphoreType.DMA,
                pltpu.SemaphoreType.DMA((nh,)),
                pltpu.SemaphoreType.DMA((nh,)),
            ],
            compiler_params=pltpu.CompilerParams(collective_id=0, has_side_effects=True),
        )(signal, b_in, c_in, step, decay_log, level_weight, skip, grad_out, state_cotangent)

    return jax.shard_map(
        on_device,
        mesh=mesh,
        in_specs=(
            P("seq", "heads"),
            P("seq", None),
            P("seq", None),
            P("heads", "seq"),
            P("heads", "seq"),
            P(None, "heads", "seq"),
            P("heads"),
            P("seq", "heads"),
            P("heads", None, None),
        ),
        out_specs=(P("seq", "heads"), P("seq", "heads"), P("seq", None), P("seq", None)),
        check_vma=False,
    )
```

```python
import functools

import jax
import jax.numpy as jnp
from jax import lax
from jax.experimental import pallas as pl
from jax.experimental.pallas import tpu as pltpu
from jax.sharding import PartitionSpec as P

MESH = pl.DeviceIdType.MESH
HIGH = lax.Precision.HIGHEST
F32 = jnp.float32
BF16 = jnp.bfloat16


def split(v):
    hi = v.astype(BF16)
    return hi, (v - hi.astype(F32)).astype(BF16)


def dot(a, b, ca, cb):
    return lax.dot_general(a, b, (((ca,), (cb,)), ((), ())), preferred_element_type=F32)


def kernel(
    n, depth, nh, heads, width,
    x_ref, b_ref, c_ref, step_ref, decay_ref, lw_ref, skip_ref, dy_ref, cot_ref,
    y_out, dx_out, db_out, dc_out,
    dself, dfar, s_buf, t1, f, tq, g, rc, gh, rx, g1, r0, cs, cr, dt,
    v_hi, v_lo, coefx, u_hi, u_lo, tsx, y_acc, dx_acc, sg, dcl, hx,
    ssem, rsem, hs_sem, hr_sem,
):
    me = lax.axis_index("seq")
    mh = lax.axis_index("heads")
    tokens = x_ref.shape[0]
    rows = b_ref.shape[1]
    half, quarter = rows // 2, rows // 4
    psize = width // heads
    core = me % 2
    xbit = (me // 2) % 2
    half_own = pl.multiple_of(core * half, half)
    half_other = pl.multiple_of((1 - core) * half, half)
    q_own = pl.multiple_of(core * half + xbit * quarter, quarter)

    def bit(k):
        return (me // (1 << k)) % 2

    def partner(k):
        return me + (1 << k) * (1 - 2 * bit(k))

    barrier = pltpu.get_barrier_semaphore()

    for k in range(depth):
        pl.semaphore_signal(barrier, inc=1, device_id={"seq": partner(k)}, device_id_type=MESH)
    for j in range(1, nh):
        pl.semaphore_signal(barrier, inc=1, device_id={"heads": (mh + j) % nh}, device_id_type=MESH)

    pending = []

    def copy(idx, src, dst, k):
        return pltpu.make_async_remote_copy(
            src_ref=src, dst_ref=dst, send_sem=ssem.at[idx], recv_sem=rsem.at[idx],
            device_id={"seq": partner(k)}, device_id_type=MESH,
        )

    names = {}

    def send(name, src, dst, k, when=None):
        idx = names.setdefault(name, len(names))
        cp = copy(idx, src, dst, k)
        pending.append((cp, when))
        if when is None:
            cp.start()
        else:
            pl.when(when)(cp.start)

    def recv(name, dst, k, when=None):
        idx = names[name]
        cp = copy(idx, dst, dst, k)
        if when is None:
            cp.wait_recv()
        else:
            pl.when(when)(cp.wait_recv)

    hpad = -(-heads // 16) * 16
    hrow = lax.broadcasted_iota(jnp.int32, (hpad, width), 0)
    hcol = lax.broadcasted_iota(jnp.int32, (hpad, width), 1)
    e1 = jnp.where((hcol >= hrow * psize) & (hcol < (hrow + 1) * psize), 1.0, 0.0).astype(BF16)
    e3 = jnp.concatenate([e1, e1, e1], axis=0)

    def pad(v):
        return jnp.concatenate([v, jnp.zeros((hpad - heads, v.shape[1]), F32)], axis=0)

    def expand(v):
        p0 = v.astype(BF16)
        rest = v - p0.astype(F32)
        p1 = rest.astype(BF16)
        p2 = (rest - p1.astype(F32)).astype(BF16)
        return dot(jnp.concatenate([p0, p1, p2], axis=0), e3, 0, 0)

    ti = lax.broadcasted_iota(jnp.int32, (tokens, tokens), 0)
    tj = lax.broadcasted_iota(jnp.int32, (tokens, tokens), 1)
    lower = ti >= tj
    step = pad(step_ref[...])
    cum = jnp.dot(pad(decay_ref[...]), jnp.where(ti <= tj, 1.0, 0.0), precision=HIGH,
                  preferred_element_type=F32)
    dself[0] = expand(cum)[tokens - 1:tokens, :]

    x = x_ref[...]
    dy = dy_ref[...]
    b = b_ref[...]
    c = c_ref[...]
    tail = jnp.exp(cum[:, tokens - 1:tokens] - cum)
    ts = expand(tail * step)
    tsx[...] = ts
    uh, ul = split(ts * x.astype(F32))
    u_hi[...] = uh
    u_lo[...] = ul
    s_buf[...] = dot(b, uh, 0, 0) + dot(b, ul, 0, 0)

    pl.semaphore_wait(barrier, depth + nh - 1)
    send(("D", 0), dself.at[0], dfar.at[0], 0)
    send("F0", s_buf, f.at[0], 0)

    up = []
    top = depth - 1
    none = jnp.zeros((1, width), F32)

    def retention_round(k):
        recv(("D", k), dfar.at[k], k)
        up.append(jnp.exp(jnp.where(bit(k) == 1, dself[k], dfar[k])))
        if k < top:
            dself[k + 1] = dself[k] + dfar[k]
            send(("D", k + 1), dself.at[k + 1], dfar.at[k + 1], k + 1)

    def before(first, last):
        total = none
        for j in range(first, last):
            total = total + jnp.where(bit(j) == 1, dfar[j], 0.0)
        return jnp.exp(total)

    def merge(k, own, far):
        is_up = bit(k) == 1
        return jnp.where(is_up, own + up[k] * far, far + up[k] * own)

    own_rows = pl.ds(half_own, half)
    own_q = pl.ds(q_own, quarter)
    side_q = pl.ds(pl.multiple_of(core * half + (1 - xbit) * quarter, quarter), quarter)
    q_in_half = pl.ds(pl.multiple_of(xbit * quarter, quarter), quarter)
    side_in_half = pl.ds(pl.multiple_of((1 - xbit) * quarter, quarter), quarter)

    retention_round(0)
    recv("F0", f.at[0], 0)
    t1[...] = merge(0, s_buf[own_rows], f[0, own_rows])
    send("F1A", t1.at[side_in_half], f.at[1, side_q], 1)

    ecum = jnp.exp(cum)

    def level_grad(k):
        @pl.when(bit(k) == 1)
        def _():
            coef = expand(pad(lw_ref[:, k, :]) * ecum)
            coefx[k] = coef
            vh, vl = split(coef * dy.astype(F32))
            v_hi[k] = vh
            v_lo[k] = vl
            g[k] = dot(c, vh, 0, 0) + dot(c, vl, 0, 0)

    order = list(range(top, 1, -1))
    for k in order:
        level_grad(k)
    retention_round(1)
    inner = before(0, 2)

    def scatter(k, scale):
        @pl.when(bit(k) == 1)
        def _():
            g[k] = g[k] * scale
        send(("RC", k), g.at[k, pl.ds(half_other, half)], rc.at[k], 0, bit(k) == 1)

    for k in order:
        scatter(k, inner)
    level_grad(1)
    scatter(1, before(0, 1))
    level_grad(0)
    send("R0", g.at[0], r0, 0, bit(0) == 1)

    def fold_core(k):
        recv(("RC", k), rc.at[k], 0, bit(k) == 1)

        @pl.when(bit(k) == 1)
        def _():
            gh[k] = g[k, own_rows] + rc[k]

    for k in order:
        fold_core(k)
        send(("RX", k), gh.at[k, side_in_half], rx.at[k], 1, bit(k) == 1)
    for k in range(2, top):
        retention_round(k)
    recv("F1A", f.at[1, own_q], 1)
    tq[2] = merge(1, t1[q_in_half], f[1, own_q])
    send(("F", 2), tq.at[2], f.at[2, own_q], 2, bit(2) == 0 if top == 2 else None)
    fold_core(1)
    send("R1X", gh.at[1], g1.at[own_rows], 1, bit(1) == 1)
    send("F1B", t1.at[q_in_half], f.at[1, own_q], 1, bit(1) == 0)

    scores = dot(c, b, 1, 1)
    cum_t = cum.T
    left = lax.broadcasted_iota(jnp.int32, (tokens, 2 * psize), 1) < psize
    zero = jnp.zeros((tokens, 2 * psize), BF16)
    sg[...] = jnp.zeros_like(sg)

    def pair(p):
        lanes = slice(p * 2 * psize, (p + 1) * 2 * psize)
        xp, dyp = x[:, lanes], dy[:, lanes]
        xs = [jnp.where(left, xp, zero), jnp.where(left, zero, xp)]
        dys = [jnp.where(left, dyp, zero), jnp.where(left, zero, dyp)]
        his, los = [], []
        total = None
        for a in range(2):
            h = 2 * p + a
            diff = cum_t[:, h:h + 1] - cum[h:h + 1, :]
            w = jnp.where(lower, jnp.exp(jnp.where(lower, diff, 0.0)), 0.0) * step[h:h + 1, :]
            part = dot(dys[a], xs[a], 1, 1) * w
            total = part if total is None else total + part
            hi, lo = split(scores * w)
            his.append(hi)
            los.append(lo)
        sg[...] += total
        xcat = jnp.concatenate(xs, axis=0)
        dycat = jnp.concatenate(dys, axis=0)
        gain = jnp.where(left[:1], skip_ref[2 * p], skip_ref[2 * p + 1])
        y_acc[:, lanes] = (
            dot(jnp.concatenate(his, axis=1), xcat, 1, 0) + dot(jnp.concatenate(los, axis=1), xcat, 1, 0)
            + gain * xp.astype(F32))
        dx_acc[:, lanes] = (
            dot(jnp.concatenate(his, axis=0), dycat, 0, 0) + dot(jnp.concatenate(los, axis=0), dycat, 0, 0)
            + gain * dyp.astype(F32))

    pairs = list(range(heads // 2))

    def some(count):
        for _ in range(count):
            if pairs:
                pair(pairs.pop(0))

    some(2)

    def level_full(k):
        recv(("FX", k), f.at[k, side_q], 1, bit(k) == 1)
        send(("FC", k), f.at[k, own_rows], f.at[k, own_rows], 0, bit(k) == 1)

    carry = None
    for r in range(2, depth):
        kb = top - (r - 2)
        recv(("RX", kb), rx.at[kb], 1, bit(kb) == 1)
        is_up = bit(kb) == 1
        grad = jnp.where(is_up, before(2, kb) * (gh[kb, q_in_half] + rx[kb]), 0.0)
        if carry is None:
            cs[kb] = grad
            send(("C", kb), cs.at[kb], cr.at[kb], kb, is_up)
        else:
            cs[kb] = jnp.where(is_up, up[kb] * carry + grad, carry)
            send(("C", kb), cs.at[kb], cr.at[kb], kb)
        some(1)
        recv(("F", r), f.at[r, own_q], r, bit(r) == 1 if r == top else None)
        if r < top:
            tq[r + 1] = merge(r, tq[r], f[r, own_q])
            send(("F", r + 1), tq.at[r + 1], f.at[r + 1, own_q], r + 1, bit(r + 1) == 0 if r + 1 == top else None)
        send(("FX", r), f.at[r, own_q], f.at[r, own_q], 1, bit(r) == 1)
        if r > 2:
            level_full(r - 1)
        recv(("C", kb), cr.at[kb], kb, bit(kb) == 0 if kb == top else None)
        if carry is None:
            carry = jnp.where(is_up, 0.0, cr[kb])
        else:
            carry = jnp.where(is_up, carry, up[kb] * carry) + cr[kb]
    has_carry = (me // 4) != (n // 4 - 1)

    @pl.when(has_carry)
    def _():
        dt[own_q] = carry

    @pl.when(jnp.logical_not(has_carry))
    def _():
        dt[...] = jnp.zeros_like(dt)

    send("CX", dt.at[own_q], dt.at[own_q], 1, has_carry)
    recv("F1B", f.at[1, side_q], 1, bit(1) == 1)
    send("F1C", f.at[1, own_rows], f.at[1, own_rows], 0, bit(1) == 1)
    recv("R1X", g1.at[own_rows], 1, bit(1) == 0)
    send("R1A", g1.at[own_rows], g1.at[own_rows], 0, bit(1) == 0)
    some(len(pairs))
    dcl[...] = dot(split(sg[...])[0], b, 1, 0) + dot(split(sg[...])[1], b, 1, 0)

    def use_level(k):
        @pl.when(bit(k) == 1)
        def _():
            level = f[k] if k == 0 else f[k] * before(0, k)
            lh, ll = split(level)
            y_acc[...] += coefx[k] * (dot(c, lh, 1, 0) + dot(c, ll, 1, 0))
            vh, vl = v_hi[k], v_lo[k]
            dcl[...] += dot(vh, lh, 1, 1) + dot(vh, ll, 1, 1) + dot(vl, lh, 1, 1)

    use_level(0)
    level_full(top)
    recv("F1C", f.at[1, pl.ds(half_other, half)], 0, bit(1) == 1)
    use_level(1)
    recv("CX", dt.at[side_q], 1, has_carry)
    send("CC", dt.at[own_rows], dt.at[own_rows], 0, has_carry)
    for k in range(2, depth):
        recv(("FC", k), f.at[k, pl.ds(half_other, half)], 0, bit(k) == 1)
        use_level(k)

    def head_copy(j, part):
        return pltpu.make_async_remote_copy(
            src_ref=hx.at[mh, part], dst_ref=hx.at[mh, part],
            send_sem=hs_sem.at[j, part], recv_sem=hr_sem.at[j, part],
            device_id={"heads": (mh + j) % nh}, device_id_type=MESH,
        )

    hx[mh, 0] = dcl[...]
    for j in range(1, nh):
        head_copy(j, 0).start()
    y_out[...] = y_acc[...].astype(BF16)

    recv("R1A", g1.at[pl.ds(half_other, half)], 0, bit(1) == 0)
    recv("R0", r0, 0, bit(0) == 0)
    recv("CC", dt.at[pl.ds(half_other, half)], 0, has_carry)
    retention_round(top)
    cot = jnp.concatenate(
        [jnp.concatenate([cot_ref[2 * p], cot_ref[2 * p + 1]], axis=0).T for p in range(heads // 2)], axis=1)
    ds_ = dt[...]
    ds_ = jnp.where(bit(1) == 1, ds_, up[1] * ds_ + g1[...])
    ds_ = jnp.where(bit(0) == 1, ds_, up[0] * ds_ + r0[...])
    later = none
    for j in range(depth):
        later = later + jnp.where(bit(j) == 0, dfar[j], 0.0)
    ds_ = ds_ + jnp.exp(later) * cot
    dh, dl = split(ds_)
    uh, ul = u_hi[...], u_lo[...]
    sh, sl = split(sg[...])
    hx[mh, 1] = (dot(sh, c, 0, 0) + dot(sl, c, 0, 0)
                 + dot(uh, dh, 1, 1) + dot(uh, dl, 1, 1) + dot(ul, dh, 1, 1))

    for j in range(1, nh):
        head_copy(j, 1).start()
    dx_out[...] = (dx_acc[...] + tsx[...] * (dot(b, dh, 1, 0) + dot(b, dl, 1, 0))).astype(BF16)
    for j in range(1, nh):
        head_copy(j, 0).wait_recv()
        head_copy(j, 1).wait_recv()
    dc, db = hx[0, 0], hx[0, 1]
    for v in range(1, nh):
        dc = dc + hx[v, 0]
        db = db + hx[v, 1]
    dc_out[...] = dc.astype(BF16)
    db_out[...] = db.astype(BF16)
    for j in range(1, nh):
        head_copy(j, 0).wait_send()
        head_copy(j, 1).wait_send()
    for cp, when in pending:
        if when is None:
            cp.wait_send()
        else:
            pl.when(when)(cp.wait_send)


def hand_over(*refs):
    for src, dst in zip(refs[:4], refs[4:]):
        dst[...] = src[...]


def solution(mesh):
    n, nh = mesh.shape["seq"], mesh.shape["heads"]
    depth = n.bit_length() - 1

    def on_device(signal, b_in, c_in, step, decay_log, level_weight, skip, grad_out, state_cotangent):
        tokens, width = signal.shape
        heads = step.shape[0]
        rows = b_in.shape[1]
        half, quarter = rows // 2, rows // 4
        vm = lambda shape, dtype=F32: pltpu.VMEM(shape, dtype)
        count = 16 + 8 * depth
        spec = pl.BlockSpec(memory_space=pltpu.VMEM)
        results = pl.pallas_call(
            functools.partial(kernel, n, depth, nh, heads, width),
            name="loglinear",
            out_shape=(
                jax.ShapeDtypeStruct((tokens, width), BF16),
                jax.ShapeDtypeStruct((tokens, width), BF16),
                jax.ShapeDtypeStruct((tokens, rows), BF16),
                jax.ShapeDtypeStruct((tokens, rows), BF16),
            ),
            in_specs=[spec] * 6 + [pl.BlockSpec(memory_space=pltpu.SMEM)] + [spec] * 2,
            out_specs=(spec,) * 4,
            scratch_shapes=[
                vm((depth, 1, width)),
                vm((depth, 1, width)),
                vm((rows, width)),
                vm((half, width)),
                vm((depth, rows, width)),
                vm((depth, quarter, width)),
                vm((depth, rows, width)),
                vm((depth, half, width)),
                vm((depth, half, width)),
                vm((depth, quarter, width)),
                vm((rows, width)),
                vm((rows, width)),
                vm((depth, quarter, width)),
                vm((depth, quarter, width)),
                vm((rows, width)),
                vm((depth, tokens, width), BF16),
                vm((depth, tokens, width), BF16),
                vm((depth, tokens, width)),
                vm((tokens, width), BF16),
                vm((tokens, width), BF16),
                vm((tokens, width)),
                vm((tokens, width)),
                vm((tokens, width)),
                vm((tokens, tokens)),
                vm((tokens, rows)),
                vm((nh, 2, tokens, rows)),
                pltpu.SemaphoreType.DMA((count,)),
                pltpu.SemaphoreType.DMA((count,)),
                pltpu.SemaphoreType.DMA((nh, 2)),
                pltpu.SemaphoreType.DMA((nh, 2)),
            ],
            compiler_params=pltpu.CompilerParams(collective_id=0, has_side_effects=True),
        )(signal, b_in, c_in, step, decay_log, level_weight.transpose(1, 0, 2), skip, grad_out,
          state_cotangent.transpose(0, 2, 1))
        return pl.pallas_call(
            hand_over,
            name="handover",
            out_shape=tuple(jax.ShapeDtypeStruct(r.shape, r.dtype) for r in results),
            in_specs=[spec] * 4,
            out_specs=(spec,) * 4,
        )(*results)

    return jax.shard_map(
        on_device,
        mesh=mesh,
        in_specs=(
            P("seq", "heads"),
            P("seq", None),
            P("seq", None),
            P("heads", "seq"),
            P("heads", "seq"),
            P(None, "heads", "seq"),
            P("heads"),
            P("seq", "heads"),
            P("heads", None, None),
        ),
        out_specs=(P("seq", "heads"), P("seq", "heads"), P("seq", None), P("seq", None)),
        check_vma=False,
    )
```

```python
import functools

import jax
import jax.numpy as jnp
from jax import lax
from jax.experimental import pallas as pl
from jax.experimental.pallas import tpu as pltpu
from jax.sharding import PartitionSpec as P

MESH = pl.DeviceIdType.MESH
HIGH = lax.Precision.HIGHEST
F32 = jnp.float32
BF16 = jnp.bfloat16
CHUNKS = 2


def split(v):
    hi = v.astype(BF16)
    return hi, (v - hi.astype(F32)).astype(BF16)


def dot(a, b, ca, cb):
    return lax.dot_general(a, b, (((ca,), (cb,)), ((), ())), preferred_element_type=F32)


def kernel(
    n, depth, nh, heads, width,
    x_ref, b_ref, c_ref, step_ref, decay_ref, lw_ref, skip_ref, dy_ref, cot_ref,
    y_out, dx_out, db_out, dc_out,
    dself, dfar, s_buf, t1, f, tq, g, rc, gh, rx, g1, r0, cs, cr, dt,
    v_hi, v_lo, coefx, u_hi, u_lo, tsx, y_acc, dx_acc, sg, dcl, hx,
    ssem, rsem, hs_sem, hr_sem,
):
    me = lax.axis_index("seq")
    mh = lax.axis_index("heads")
    tokens = x_ref.shape[0]
    rows = b_ref.shape[1]
    half, quarter = rows // 2, rows // 4
    psize = width // heads
    core = me % 2
    xbit = (me // 2) % 2
    half_own = pl.multiple_of(core * half, half)
    half_other = pl.multiple_of((1 - core) * half, half)
    q_own = pl.multiple_of(core * half + xbit * quarter, quarter)

    def bit(k):
        return (me // (1 << k)) % 2

    def partner(k):
        return me + (1 << k) * (1 - 2 * bit(k))

    barrier = pltpu.get_barrier_semaphore()

    for k in range(depth):
        pl.semaphore_signal(barrier, inc=1, device_id={"seq": partner(k)}, device_id_type=MESH)
    for j in range(1, nh):
        pl.semaphore_signal(barrier, inc=1, device_id={"heads": (mh + j) % nh}, device_id_type=MESH)

    pending = []

    def copy(idx, src, dst, k):
        return pltpu.make_async_remote_copy(
            src_ref=src, dst_ref=dst, send_sem=ssem.at[idx], recv_sem=rsem.at[idx],
            device_id={"seq": partner(k)}, device_id_type=MESH,
        )

    names = {}

    def send(name, src, dst, k, when=None):
        idx = names.setdefault(name, len(names))
        cp = copy(idx, src, dst, k)
        pending.append((cp, when))
        if when is None:
            cp.start()
        else:
            pl.when(when)(cp.start)

    def recv(name, dst, k, when=None):
        idx = names[name]
        cp = copy(idx, dst, dst, k)
        if when is None:
            cp.wait_recv()
        else:
            pl.when(when)(cp.wait_recv)

    hpad = -(-heads // 16) * 16
    hrow = lax.broadcasted_iota(jnp.int32, (hpad, width), 0)
    hcol = lax.broadcasted_iota(jnp.int32, (hpad, width), 1)
    e1 = jnp.where((hcol >= hrow * psize) & (hcol < (hrow + 1) * psize), 1.0, 0.0).astype(BF16)
    e3 = jnp.concatenate([e1, e1, e1], axis=0)

    def pad(v):
        return jnp.concatenate([v, jnp.zeros((hpad - heads, v.shape[1]), F32)], axis=0)

    def expand(v):
        p0 = v.astype(BF16)
        rest = v - p0.astype(F32)
        p1 = rest.astype(BF16)
        p2 = (rest - p1.astype(F32)).astype(BF16)
        return dot(jnp.concatenate([p0, p1, p2], axis=0), e3, 0, 0)

    ti = lax.broadcasted_iota(jnp.int32, (tokens, tokens), 0)
    tj = lax.broadcasted_iota(jnp.int32, (tokens, tokens), 1)
    lower = ti >= tj
    step = pad(step_ref[...])
    cum = jnp.dot(pad(decay_ref[...]), jnp.where(ti <= tj, 1.0, 0.0), precision=HIGH,
                  preferred_element_type=F32)
    dself[0] = expand(cum)[tokens - 1:tokens, :]

    x = x_ref[...]
    dy = dy_ref[...]
    b = b_ref[...]
    c = c_ref[...]
    ecum = jnp.exp(cum)
    top = depth - 1
    order = list(range(top, 1, -1))

    def level_grad(k):
        @pl.when(bit(k) == 1)
        def _():
            coef = expand(pad(lw_ref[:, k, :]) * ecum)
            coefx[k] = coef
            vh, vl = split(coef * dy.astype(F32))
            v_hi[k] = vh
            v_lo[k] = vl
            g[k] = dot(c, vh, 0, 0) + dot(c, vl, 0, 0)

    for k in order:
        level_grad(k)
    tail = jnp.exp(cum[:, tokens - 1:tokens] - cum)
    ts = expand(tail * step)
    tsx[...] = ts
    uh, ul = split(ts * x.astype(F32))
    u_hi[...] = uh
    u_lo[...] = ul
    s_buf[...] = dot(b, uh, 0, 0) + dot(b, ul, 0, 0)

    pl.semaphore_wait(barrier, depth + nh - 1)
    send(("D", 0), dself.at[0], dfar.at[0], 0)
    send(("RC", top), g.at[top, pl.ds(half_other, half)], rc.at[top], 0, bit(top) == 1)
    send("F0", s_buf, f.at[0], 0)
    for k in order[1:] + [1]:
        if k == 1:
            level_grad(1)
        send(("RC", k), g.at[k, pl.ds(half_other, half)], rc.at[k], 0, bit(k) == 1)
    level_grad(0)
    send("R0", g.at[0], r0, 0, bit(0) == 1)

    up = []
    down = []
    none = jnp.zeros((1, width), F32)

    def retention_round(k):
        recv(("D", k), dfar.at[k], k)
        up.append(jnp.exp(jnp.where(bit(k) == 1, dself[k], dfar[k])))
        down.append(jnp.exp(jnp.where(bit(k) == 1, dfar[k], dself[k])))
        if k < top:
            dself[k + 1] = dself[k] + dfar[k]
            send(("D", k + 1), dself.at[k + 1], dfar.at[k + 1], k + 1)

    def before(first, last):
        total = none
        for j in range(first, last):
            total = total + jnp.where(bit(j) == 1, dfar[j], 0.0)
        return jnp.exp(total)

    def merge(k, own, far):
        is_up = bit(k) == 1
        return jnp.where(is_up, own + up[k] * far, far + up[k] * own)

    def unmerge(k, own, far):
        is_up = bit(k) == 1
        return jnp.where(is_up, own * down[k] + far, own + far * down[k])

    sub = quarter // CHUNKS
    chunks = range(CHUNKS)

    def piece(start, m):
        return pl.ds(pl.multiple_of(start + m * sub, sub), sub)

    own_in, side_in = xbit * quarter, (1 - xbit) * quarter
    own_start, side_start = core * half + own_in, core * half + side_in
    own_rows = pl.ds(half_own, half)
    own_q = pl.ds(q_own, quarter)
    side_q = pl.ds(pl.multiple_of(core * half + (1 - xbit) * quarter, quarter), quarter)
    q_in_half = pl.ds(pl.multiple_of(xbit * quarter, quarter), quarter)

    retention_round(0)

    def fold_core(k):
        recv(("RC", k), rc.at[k], 0, bit(k) == 1)

        @pl.when(bit(k) == 1)
        def _():
            gh[k] = unmerge(0, g[k, own_rows], rc[k])

    def send_side(k):
        for m in chunks:
            send(("RX", k, m), gh.at[k, piece(side_in, m)], rx.at[k, pl.ds(m * sub, sub)], 1, bit(k) == 1)

    fold_core(top)
    send_side(top)
    recv("F0", f.at[0], 0)
    t1[...] = merge(0, s_buf[own_rows], f[0, own_rows])
    for m in chunks:
        send(("F1A", m), t1.at[piece(side_in, m)], f.at[1, piece(side_start, m)], 1)
    for k in order[1:]:
        fold_core(k)
        send_side(k)
    retention_round(1)
    for k in range(2, top):
        retention_round(k)

    scores = dot(c, b, 1, 1)
    cum_t = cum.T
    left = lax.broadcasted_iota(jnp.int32, (tokens, 2 * psize), 1) < psize
    zero = jnp.zeros((tokens, 2 * psize), BF16)
    sg[...] = jnp.zeros_like(sg)

    def pair(p):
        lanes = slice(p * 2 * psize, (p + 1) * 2 * psize)
        xp, dyp = x[:, lanes], dy[:, lanes]
        xs = [jnp.where(left, xp, zero), jnp.where(left, zero, xp)]
        dys = [jnp.where(left, dyp, zero), jnp.where(left, zero, dyp)]
        his, los = [], []
        total = None
        for a in range(2):
            h = 2 * p + a
            diff = cum_t[:, h:h + 1] - cum[h:h + 1, :]
            w = jnp.where(lower, jnp.exp(jnp.where(lower, diff, 0.0)), 0.0) * step[h:h + 1, :]
            part = dot(dys[a], xs[a], 1, 1) * w
            total = part if total is None else total + part
            hi, lo = split(scores * w)
            his.append(hi)
            los.append(lo)
        sg[...] += total
        xcat = jnp.concatenate(xs, axis=0)
        dycat = jnp.concatenate(dys, axis=0)
        gain = jnp.where(left[:1], skip_ref[2 * p], skip_ref[2 * p + 1])
        y_acc[:, lanes] = (
            dot(jnp.concatenate(his, axis=1), xcat, 1, 0) + dot(jnp.concatenate(los, axis=1), xcat, 1, 0)
            + gain * xp.astype(F32))
        dx_acc[:, lanes] = (
            dot(jnp.concatenate(his, axis=0), dycat, 0, 0) + dot(jnp.concatenate(los, axis=0), dycat, 0, 0)
            + gain * dyp.astype(F32))

    pairs = list(range(heads // 2))

    def some(count):
        for _ in range(count):
            if pairs:
                pair(pairs.pop(0))

    some(1)

    def send_level(k, m, own, far):
        tq[k, pl.ds(m * sub, sub)] = merge(k - 1, own, far)
        send(("F", k, m), tq.at[k, pl.ds(m * sub, sub)], f.at[k, piece(own_start, m)], k,
             bit(k) == 0 if k == top else None)

    carry = [None] * CHUNKS

    def start_carry(k, m):
        rows_m = pl.ds(m * sub, sub)
        recv(("RX", k, m), rx.at[k, rows_m], 1, bit(k) == 1)
        is_up = bit(k) == 1
        grad = jnp.where(is_up, before(2, k) * unmerge(1, gh[k, piece(own_in, m)], rx[k, rows_m]), 0.0)
        if k == top:
            cs[k, rows_m] = grad
        else:
            cs[k, rows_m] = jnp.where(is_up, up[k] * carry[m] + grad, carry[m])
        send(("C", k, m), cs.at[k, rows_m], cr.at[k, rows_m], k, is_up if k == top else None)

    def end_carry(k, m):
        rows_m = pl.ds(m * sub, sub)
        recv(("C", k, m), cr.at[k, rows_m], k, bit(k) == 0 if k == top else None)
        is_up = bit(k) == 1
        if k == top:
            carry[m] = jnp.where(is_up, 0.0, cr[k, rows_m])
        else:
            carry[m] = jnp.where(is_up, carry[m], up[k] * carry[m]) + cr[k, rows_m]

    for m in chunks:
        start_carry(top, m)
    for m in chunks:
        recv(("F1A", m), f.at[1, piece(own_start, m)], 1)
        send_level(2, m, t1[piece(own_in, m)], f[1, piece(own_start, m)])
    fold_core(1)
    send("R1X", gh.at[1], g1.at[own_rows], 1, bit(1) == 1)
    send("F1B", t1.at[q_in_half], f.at[1, own_q], 1, bit(1) == 0)
    has_carry = (me // 4) != (n // 4 - 1)

    @pl.when(jnp.logical_not(has_carry))
    def _():
        dt[...] = jnp.zeros_like(dt)

    def level_full(k):
        for m in chunks:
            recv(("FX", k, m), f.at[k, piece(side_start, m)], 1, bit(k) == 1)
        send(("FC", k), f.at[k, own_rows], f.at[k, own_rows], 0, bit(k) == 1)

    def forward_round(r):
        for m in chunks:
            here = f.at[r, piece(own_start, m)]
            recv(("F", r, m), here, r, bit(r) == 1 if r == top else None)
            if r < top:
                send_level(r + 1, m, tq[r, pl.ds(m * sub, sub)], f[r, piece(own_start, m)])
            send(("FX", r, m), here, here, 1, bit(r) == 1)
        if r > 2:
            level_full(r - 1)

    def store_carry(m):
        @pl.when(has_carry)
        def _():
            dt[piece(own_start, m)] = carry[m]
        send(("CX", m), dt.at[piece(own_start, m)], dt.at[piece(own_start, m)], 1, has_carry)

    def backward_round(k):
        for m in chunks:
            end_carry(k, m)
            if k > 2:
                start_carry(k - 1, m)
            else:
                store_carry(m)

    for r in range(2, depth):
        some(1)
        if r < top:
            forward_round(r)
            backward_round(top + 2 - r)
        else:
            backward_round(top + 2 - r)
            forward_round(r)
    recv("F1B", f.at[1, side_q], 1, bit(1) == 1)
    send("F1C", f.at[1, own_rows], f.at[1, own_rows], 0, bit(1) == 1)
    recv("R1X", g1.at[own_rows], 1, bit(1) == 0)
    send("R1A", g1.at[own_rows], g1.at[own_rows], 0, bit(1) == 0)
    some(len(pairs))
    dcl[...] = dot(split(sg[...])[0], b, 1, 0) + dot(split(sg[...])[1], b, 1, 0)

    def use_level(k):
        @pl.when(bit(k) == 1)
        def _():
            level = f[k] if k == 0 else f[k] * before(0, k)
            lh, ll = split(level)
            y_acc[...] += coefx[k] * (dot(c, lh, 1, 0) + dot(c, ll, 1, 0))
            vh, vl = v_hi[k], v_lo[k]
            dcl[...] += dot(vh, lh, 1, 1) + dot(vh, ll, 1, 1) + dot(vl, lh, 1, 1)

    use_level(0)
    level_full(top)
    recv("F1C", f.at[1, pl.ds(half_other, half)], 0, bit(1) == 1)
    use_level(1)
    for m in chunks:
        recv(("CX", m), dt.at[piece(side_start, m)], 1, has_carry)
    send("CC", dt.at[own_rows], dt.at[own_rows], 0, has_carry)
    for k in range(2, depth):
        recv(("FC", k), f.at[k, pl.ds(half_other, half)], 0, bit(k) == 1)
        use_level(k)

    def head_copy(j, part):
        return pltpu.make_async_remote_copy(
            src_ref=hx.at[mh, part], dst_ref=hx.at[mh, part],
            send_sem=hs_sem.at[j, part], recv_sem=hr_sem.at[j, part],
            device_id={"heads": (mh + j) % nh}, device_id_type=MESH,
        )

    hx[mh, 0] = dcl[...]
    for j in range(1, nh):
        head_copy(j, 0).start()
    y_out[...] = y_acc[...].astype(BF16)

    recv("R1A", g1.at[pl.ds(half_other, half)], 0, bit(1) == 0)
    recv("R0", r0, 0, bit(0) == 0)
    recv("CC", dt.at[pl.ds(half_other, half)], 0, has_carry)
    retention_round(top)
    cot = jnp.concatenate(
        [jnp.concatenate([cot_ref[2 * p], cot_ref[2 * p + 1]], axis=0).T for p in range(heads // 2)], axis=1)
    ds_ = dt[...]
    ds_ = jnp.where(bit(1) == 1, ds_, up[1] * ds_ + g1[...])
    ds_ = jnp.where(bit(0) == 1, ds_, up[0] * ds_ + r0[...])
    later = none
    for j in range(depth):
        later = later + jnp.where(bit(j) == 0, dfar[j], 0.0)
    ds_ = ds_ + jnp.exp(later) * cot
    dh, dl = split(ds_)
    uh, ul = u_hi[...], u_lo[...]
    sh, sl = split(sg[...])
    hx[mh, 1] = (dot(sh, c, 0, 0) + dot(sl, c, 0, 0)
                 + dot(uh, dh, 1, 1) + dot(uh, dl, 1, 1) + dot(ul, dh, 1, 1))

    for j in range(1, nh):
        head_copy(j, 1).start()
    dx_out[...] = (dx_acc[...] + tsx[...] * (dot(b, dh, 1, 0) + dot(b, dl, 1, 0))).astype(BF16)
    for j in range(1, nh):
        head_copy(j, 0).wait_recv()
        head_copy(j, 1).wait_recv()
    dc, db = hx[0, 0], hx[0, 1]
    for v in range(1, nh):
        dc = dc + hx[v, 0]
        db = db + hx[v, 1]
    dc_out[...] = dc.astype(BF16)
    db_out[...] = db.astype(BF16)
    for j in range(1, nh):
        head_copy(j, 0).wait_send()
        head_copy(j, 1).wait_send()
    for cp, when in pending:
        if when is None:
            cp.wait_send()
        else:
            pl.when(when)(cp.wait_send)


def hand_over(*refs):
    for src, dst in zip(refs[:4], refs[4:]):
        dst[...] = src[...]


def solution(mesh):
    n, nh = mesh.shape["seq"], mesh.shape["heads"]
    depth = n.bit_length() - 1

    def on_device(signal, b_in, c_in, step, decay_log, level_weight, skip, grad_out, state_cotangent):
        tokens, width = signal.shape
        heads = step.shape[0]
        rows = b_in.shape[1]
        half, quarter = rows // 2, rows // 4
        vm = lambda shape, dtype=F32: pltpu.VMEM(shape, dtype)
        count = 16 + 4 * CHUNKS + (4 + 4 * CHUNKS) * depth
        spec = pl.BlockSpec(memory_space=pltpu.VMEM)
        results = pl.pallas_call(
            functools.partial(kernel, n, depth, nh, heads, width),
            name="loglinear",
            out_shape=(
                jax.ShapeDtypeStruct((tokens, width), BF16),
                jax.ShapeDtypeStruct((tokens, width), BF16),
                jax.ShapeDtypeStruct((tokens, rows), BF16),
                jax.ShapeDtypeStruct((tokens, rows), BF16),
            ),
            in_specs=[spec] * 6 + [pl.BlockSpec(memory_space=pltpu.SMEM)] + [spec] * 2,
            out_specs=(spec,) * 4,
            scratch_shapes=[
                vm((depth, 1, width)),
                vm((depth, 1, width)),
                vm((rows, width)),
                vm((half, width)),
                vm((depth, rows, width)),
                vm((depth, quarter, width)),
                vm((depth, rows, width)),
                vm((depth, half, width)),
                vm((depth, half, width)),
                vm((depth, quarter, width)),
                vm((rows, width)),
                vm((rows, width)),
                vm((depth, quarter, width)),
                vm((depth, quarter, width)),
                vm((rows, width)),
                vm((depth, tokens, width), BF16),
                vm((depth, tokens, width), BF16),
                vm((depth, tokens, width)),
                vm((tokens, width), BF16),
                vm((tokens, width), BF16),
                vm((tokens, width)),
                vm((tokens, width)),
                vm((tokens, width)),
                vm((tokens, tokens)),
                vm((tokens, rows)),
                vm((nh, 2, tokens, rows)),
                pltpu.SemaphoreType.DMA((count,)),
                pltpu.SemaphoreType.DMA((count,)),
                pltpu.SemaphoreType.DMA((nh, 2)),
                pltpu.SemaphoreType.DMA((nh, 2)),
            ],
            compiler_params=pltpu.CompilerParams(collective_id=0, has_side_effects=True),
        )(signal, b_in, c_in, step, decay_log, level_weight.transpose(1, 0, 2), skip, grad_out,
          state_cotangent.transpose(0, 2, 1))
        return pl.pallas_call(
            hand_over,
            name="handover",
            out_shape=tuple(jax.ShapeDtypeStruct(r.shape, r.dtype) for r in results),
            in_specs=[spec] * 4,
            out_specs=(spec,) * 4,
        )(*results)

    return jax.shard_map(
        on_device,
        mesh=mesh,
        in_specs=(
            P("seq", "heads"),
            P("seq", None),
            P("seq", None),
            P("heads", "seq"),
            P("heads", "seq"),
            P(None, "heads", "seq"),
            P("heads"),
            P("seq", "heads"),
            P("heads", None, None),
        ),
        out_specs=(P("seq", "heads"), P("seq", "heads"), P("seq", None), P("seq", None)),
        check_vma=False,
    )
```
